32 devices in a mesh: gx: 4 (over z), gy: 4 (over y, x), gz: 2 (over core).
Axes of the slice: x: 2, y: 2, z: 4, core: 2. Of those that a mesh axis runs over, the one named last changes fastest.
Arguments:
- params: float32 [59, 65536], P(None, ('gx', 'gy', 'gz')), may hold values from -6 to 6
- gradients: float32 [59, 65536], P(None, ('gx', 'gy', 'gz')), may hold values from -80 to 80
- moment_one: float32 [59, 65536], P(None, ('gx', 'gy', 'gz')), may hold values from -4 to 4
- moment_two: float32 [59, 65536], P(None, ('gx', 'gy', 'gz')), may hold values from 0.01 to 1
- keep_mask: int32 [65536], P(('gx', 'gy', 'gz')), may hold values from 0 to 1, as said below
Outputs:
- new_params: float32 [59, 65536], P(None, ('gx', 'gy', 'gz'))
- new_moment_one: float32 [59, 65536], P(None, ('gx', 'gy', 'gz'))
- new_moment_two: float32 [59, 65536], P(None, ('gx', 'gy', 'gz'))
- grad_rms: float32 [], replicated
The draws below stay inside these ranges and needn't reach their ends.
Inputs may be any that keep to these rules, and one draw needn't show every extreme that they name: `keep_mask`: exactly 32 of the blocks of 128 aligned columns hold no 1; every other block holds at least one.
All inputs are finite; a program needn't handle non-finite values.
Results may differ from the reference program's by a relative error of at most 0.000067.
Values sent between devices are 32-bit elements; how exact they have to be, the bound alone decides.
A program may use at most 64 MiB of HBM per device.

```python
import math
import jax
import jax.numpy as jnp
from jax import lax

FEATURES = 59
BLOCK = 128
STEP = 10
ROWS_DEV = 2048
ROWS = 65536
DROPS = 32


def draw_gradients(key, part):
    first_key, second_key = jax.random.split(jax.random.fold_in(key, 11), 2)
    position = jnp.arange(ROWS, dtype=jnp.float32) / ROWS
    rough = jnp.exp(jax.random.uniform(second_key, (ROWS,), jnp.float32, -0.7, 0.7))
    values = jax.random.truncated_normal(first_key, -4.0, 4.0, (FEATURES, ROWS), jnp.float32)
    scale = jnp.exp(jnp.log(3.0) * position) * rough
    return (values * scale[None, :]).astype(jnp.float32)


def draw_keep_mask(key, part):
    first_key, second_key, third_key, fourth_key, fifth_key = jax.random.split(jax.random.fold_in(key, 23), 5)
    total_blocks = ROWS // BLOCK
    blocks_dev = ROWS_DEV // BLOCK
    device_count = ROWS // ROWS_DEV
    ordering = jax.random.permutation(first_key, total_blocks).astype(jnp.int32)
    first_block = jax.random.randint(fourth_key, (), 0, blocks_dev).astype(jnp.int32)
    middle_block = (device_count // 2 * blocks_dev + jax.random.randint(fifth_key, (), 0, blocks_dev)).astype(jnp.int32)
    held = ordering[first_block]
    ordering = jnp.where(ordering == 0, held, ordering)
    ordering = ordering.at[first_block].set(0)
    held = ordering[middle_block]
    ordering = jnp.where(ordering == 1, held, ordering)
    ordering = ordering.at[middle_block].set(1)
    emptied = ordering < DROPS
    coins = jax.random.randint(second_key, (total_blocks, BLOCK), 0, 10) < 7
    chosen = jax.random.randint(third_key, (total_blocks, 1), 0, BLOCK)
    within = jnp.arange(BLOCK, dtype=jnp.int32)[None, :]
    survive = (coins | (within == chosen)) & jnp.logical_not(emptied)[:, None]
    return survive.astype(jnp.int32).reshape(ROWS)


def block_scale(stream_key, shape, cuts, low, top_value):
    def one(axis_at, blocks):
        heights = jax.random.uniform(jax.random.fold_in(jax.random.fold_in(stream_key, 6), axis_at), (blocks,), jnp.float32, low / len(cuts), top_value / len(cuts))
        return jnp.repeat(jnp.exp(heights), shape[axis_at] // blocks).reshape((-1,) + (1,) * (len(shape) - axis_at - 1))

    gain = one(*cuts[0])
    for cut in cuts[1:]:
        gain = gain * one(*cut)
    return gain


def scatter_about(rng, dims, scale, limit, shards=(), kind=jnp.bfloat16):
    values = jax.random.normal(rng, dims, jnp.float32) * scale
    if len(shards) > 0:
        values = block_scale(rng, dims, shards, -0.22, 0.18) * values
    return jnp.clip(values, min=-limit, max=limit).astype(kind)


def setup_inputs(seed: int = 0) -> dict:
    keys = jax.random.split(jax.random.key(seed), 6)
    return {
        "params": scatter_about(keys[0], (FEATURES, ROWS), 1.0, 6.0, ((1, 32),), jnp.float32),
        "gradients": draw_gradients(jax.random.fold_in(keys[5], 71), 0),
        "moment_one": scatter_about(keys[2], (FEATURES, ROWS), 0.3, 4.0, ((1, 32),), jnp.float32),
        "moment_two": jnp.clip(jnp.exp(math.log(1.0) - 4.6051702 * jax.random.uniform(keys[3], (FEATURES, ROWS), jnp.float32) ** block_scale(keys[3], (FEATURES, ROWS), ((1, 32),), -0.2, 0.2)), 0.01, 1.0),
        "keep_mask": draw_keep_mask(jax.random.fold_in(keys[5], 71), 0),
    }


beta_one = 0.9
beta_two = 0.999
learn_rate = 0.05
adam_eps = 1e-08
clip_rms = 1.0

def adam_update(params, gradients, moment_one, moment_two, clip_factor):
    clipped = clip_factor * gradients
    first = beta_one * moment_one + (1.0 - beta_one) * clipped
    second = beta_two * moment_two + (1.0 - beta_two) * clipped * clipped
    correct_one = 1.0 - beta_one ** STEP
    correct_two = 1.0 - beta_two ** STEP
    updated = params - learn_rate * (first / correct_one) / (jnp.sqrt(second / correct_two) + adam_eps)
    return (updated, first, second)

def reference(params, gradients, moment_one, moment_two, keep_mask):
    square_total = jnp.sum(gradients * gradients)
    grad_rms = jnp.sqrt(square_total / (FEATURES * ROWS))
    clip_factor = jnp.minimum(1.0, clip_rms / (grad_rms + 1e-06))
    updated, first, second = adam_update(params, gradients, moment_one, moment_two, clip_factor)
    stacked = jnp.stack([updated, first, second])
    stacked = jnp.where(keep_mask[None, None, :] > 0, stacked, 0.0)
    total_blocks = ROWS // BLOCK
    counts = lax.optimization_barrier(jnp.sum(keep_mask.reshape(total_blocks, BLOCK), axis=1))
    block_alive = (counts > 0).astype(jnp.int32)
    block_rank = (jnp.cumsum(block_alive) - block_alive).astype(jnp.int32)
    target_block = jnp.where(block_alive > 0, block_rank, total_blocks).astype(jnp.int32)
    blocked = stacked.reshape(3, FEATURES, total_blocks, BLOCK)
    result = jnp.zeros_like(blocked).at[:, :, target_block].set(blocked, mode='drop')
    result = result.reshape(3, FEATURES, ROWS)
    return (result[0], result[1], result[2], grad_rms)
```

```python
import functools

import jax
import jax.numpy as jnp
from jax import lax
from jax.experimental import pallas as pl
from jax.experimental.pallas import tpu as pltpu
from jax.sharding import PartitionSpec as P

BLOCK = 128
DROPS = 32
STEP = 10
AXES = ("gx", "gy", "gz")
MESH = pl.DeviceIdType.MESH

beta_one = 0.9
beta_two = 0.999
learn_rate = 0.05
adam_eps = 1e-08
clip_rms = 1.0


def kernel(
    sizes, pieces, p_hbm, g_hbm, m_hbm, v_hbm, k_hbm, op_hbm, om_hbm, ov_hbm, rms_ref,
    windows, g_buf, m_buf, v_buf, o_p, o_m, o_v, keep, ag_x, ag_y, ag_z, ct_x, ct_y, ct_z,
    where_v, where_s, load_sem, out_sem, far_send, far_recv, near_send, near_recv,
    ag_send, ag_recv, where_sem,
):
    nx, ny, nz = sizes
    count = nx * ny * nz
    features, rows_dev = g_buf.shape
    blocks_dev = rows_dev // BLOCK
    n_piece = len(pieces)
    ix, iy, iz = (lax.axis_index(a) for a in AXES)
    me = (ix * ny + iy) * nz + iz
    odd = lax.rem(me, 2)
    is_odd = odd == 1
    is_even = odd == 0
    has_up = me + 2 < count
    has_down = me >= 2

    def place(n):
        return (lax.div(n, ny * nz), lax.rem(lax.div(n, nz), ny), lax.rem(n, nz))

    partner = place(me + 1 - 2 * odd)
    below = place(lax.rem(me + count - 2, count))
    above = place(lax.rem(me + 2, count))
    own, one, two = (pl.ds(i * rows_dev, rows_dev) for i in range(3))

    def span(piece):
        return pl.ds(pieces[piece][0], pieces[piece][1])

    def load(i, src, dst):
        return pltpu.make_async_copy(src, dst, load_sem.at[i])

    loads = [
        load(0, g_hbm, g_buf),
        load(1, k_hbm, keep.at[0]),
        load(2, m_hbm, m_buf),
        load(3, v_hbm, v_buf),
    ] + [
        load(4 + c, p_hbm.at[span(c)], windows[0][c].at[:, own]) for c in range(len(pieces))
    ]
    for c in loads:
        c.start()

    barrier = pltpu.get_barrier_semaphore()

    def greet(device):
        pl.semaphore_signal(barrier, inc=1, device_id=device, device_id_type=MESH)

    groups = (
        (iz, nz, ag_z, ct_z, lambda i: (ix, iy, i)),
        (iy, ny, ag_y, ct_y, lambda i: (ix, i, iz)),
        (ix, nx, ag_x, ct_x, lambda i: (i, iy, iz)),
    )
    greet(partner)
    for mine, size, _, _, at in groups:
        for k in range(1, size):
            greet(at(lax.rem(mine + k, size)))
    pl.when(has_down)(lambda: greet(below))
    pl.when(has_up)(lambda: greet(above))

    loads[0].wait()
    loads[1].wait()
    g = g_buf[...]
    square = jnp.sum(g * g, axis=1, keepdims=True)
    square = jnp.sum(square, axis=0, keepdims=True)
    alive = (jnp.max(keep[0], axis=1, keepdims=True) > 0).astype(jnp.int32)
    payload = jnp.broadcast_to(square, (8, BLOCK))
    tally = jnp.broadcast_to(jnp.sum(alive, axis=0, keepdims=True), (8, BLOCK))

    pl.semaphore_wait(
        barrier,
        1 + (nx - 1) + (ny - 1) + (nz - 1) + has_up.astype(jnp.int32) + has_down.astype(jnp.int32),
    )

    def far(i, src, dst):
        return pltpu.make_async_remote_copy(
            src_ref=src, dst_ref=dst, send_sem=far_send.at[i], recv_sem=far_recv.at[i],
            device_id=below, device_id_type=MESH,
        )

    def near(i, src, dst):
        return pltpu.make_async_remote_copy(
            src_ref=src, dst_ref=dst, send_sem=near_send.at[i], recv_sem=near_recv.at[i],
            device_id=partner, device_id_type=MESH,
        )

    keep_id = 3 * n_piece

    def far_copy(a, c):
        src = p_hbm.at[span(c)] if a == 0 else windows[a][c].at[:, own]
        return far(a * n_piece + c, src, windows[a][c].at[:, two])

    def near_own(a, c):
        src = p_hbm.at[span(c)] if a == 0 else windows[a][c].at[:, own]
        return near(a * n_piece + c, src, windows[a][c].at[:, one])

    def near_relay(a, c):
        return near(a * n_piece + c, windows[a][c].at[:, two], windows[a][c].at[:, one])

    far_keep = far(keep_id, k_hbm, keep.at[2])
    near_keep = near(keep_id, k_hbm, keep.at[1])
    relay_keep = near(keep_id, keep.at[2], keep.at[1])

    def send(a, c):
        pl.when(has_down)(lambda: far_copy(a, c).start())
        pl.when(is_odd)(lambda: near_own(a, c).start())

    pl.when(has_down)(far_keep.start)
    pl.when(is_odd)(near_keep.start)

    def no_keep(i):
        keep[i] = jnp.zeros((blocks_dev, BLOCK), jnp.int32)

    pl.when(jnp.logical_not(has_up))(lambda: no_keep(2))
    pl.when(jnp.logical_not(has_up) & is_odd)(lambda: no_keep(1))

    before = jnp.zeros((8, BLOCK), jnp.int32)
    flow = list(range(n_piece))
    sem_at = 0
    ag_copies = []
    for phase, (mine, size, ag, ct, at) in enumerate(groups):
        ag[mine] = payload
        ct[mine] = tally
        copies = []
        for k in range(1, size):
            for buf in (ag, ct):
                copies.append(
                    pltpu.make_async_remote_copy(
                        src_ref=buf.at[mine], dst_ref=buf.at[mine],
                        send_sem=ag_send.at[sem_at], recv_sem=ag_recv.at[sem_at],
                        device_id=at(lax.rem(mine + k, size)), device_id_type=MESH,
                    )
                )
                copies[-1].start()
                sem_at += 1
        for _ in range(1 if phase < 2 else n_piece):
            if flow:
                send(0, flow.pop(0))
        for c in copies:
            c.wait_recv()
        ag_copies += copies
        payload, tally = ag[0], ct[0]
        for i in range(1, size):
            payload, tally = payload + ag[i], tally + ct[i]
        for i in range(size):
            before = before + jnp.where(i < mine, ct[i], 0)

    grad_rms = jnp.sqrt(payload[0:1, 0:1] / float(features * rows_dev * count))
    rms_ref[...] = grad_rms
    clip_factor = jnp.minimum(1.0, clip_rms / (grad_rms + 1e-06))

    loads[2].wait()
    loads[3].wait()
    kept = keep[0]
    kept = jnp.concatenate([kept[b : b + 1, :] for b in range(blocks_dev)], axis=1) > 0
    for c in range(n_piece):
        rows = span(c)
        clipped = clip_factor * g_buf[rows, :]
        first = beta_one * m_buf[rows, :] + (1.0 - beta_one) * clipped
        windows[1][c][:, own] = jnp.where(kept, first, 0.0)
        second = beta_two * v_buf[rows, :] + (1.0 - beta_two) * clipped * clipped
        windows[2][c][:, own] = jnp.where(kept, second, 0.0)
        send(1, c)
        send(2, c)

    @pl.when(has_up)
    def _():
        far_keep.wait_recv()

    @pl.when(is_even & has_up)
    def _():
        relay_keep.start()

    pl.when(is_even | has_up)(near_keep.wait_recv)
    total_blocks = 3 * blocks_dev
    flags = [(jnp.max(keep[i], axis=1, keepdims=True) > 0).astype(jnp.int32) for i in range(3)]
    flags = jnp.concatenate(flags, axis=0)
    up_to = lax.broadcasted_iota(jnp.int32, (total_blocks, BLOCK), 0) <= lax.broadcasted_iota(
        jnp.int32, (total_blocks, BLOCK), 1
    )
    reached = jnp.sum(
        jnp.where(up_to, jnp.broadcast_to(flags, (total_blocks, BLOCK)), 0), axis=0, keepdims=True
    )
    shift = me * blocks_dev - before[0:1, :]
    slot = lax.broadcasted_iota(jnp.int32, (blocks_dev, BLOCK), 0)
    lane = lax.broadcasted_iota(jnp.int32, (blocks_dev, BLOCK), 1)
    passed = (reached <= slot + shift) & (lane < total_blocks)
    index = jnp.sum(passed.astype(jnp.int32), axis=1, keepdims=True)
    where_v[...] = jnp.broadcast_to(index, (blocks_dev, BLOCK))
    to_scalar = pltpu.make_async_copy(where_v, where_s, where_sem)
    to_scalar.start()
    to_scalar.wait()
    for c in loads[4:]:
        c.wait()

    def relay(a, c):
        @pl.when(has_up)
        def _():
            far_copy(a, c).wait_recv()

        @pl.when(is_even & has_up)
        def _():
            near_relay(a, c).start()

    for c in range(n_piece):
        relay(0, c)

    correct_one = 1.0 - beta_one**STEP
    correct_two = 1.0 - beta_two**STEP
    outs = []
    for c in range(n_piece):
        relay(1, c)
        relay(2, c)
        for a in range(3):
            pl.when(is_even | has_up)(near_own(a, c).wait_recv)
        rows = span(c)
        for j in range(blocks_dev):
            block = where_s[j, 0]
            valid = block < total_blocks
            start = jnp.where(valid, block, 0) * BLOCK
            dst = (rows, pl.ds(j * BLOCK, BLOCK))
            old, first, second = (windows[a][c][:, pl.ds(start, BLOCK)] for a in range(3))
            updated = old - learn_rate * (first / correct_one) / (
                jnp.sqrt(second / correct_two) + adam_eps
            )
            o_p[dst] = jnp.where(valid & (second > 0.0), updated, 0.0)
            o_m[dst] = jnp.where(valid, first, 0.0)
            o_v[dst] = jnp.where(valid, second, 0.0)
        for a, (buf, hbm) in enumerate(((o_p, op_hbm), (o_m, om_hbm), (o_v, ov_hbm))):
            outs.append(
                pltpu.make_async_copy(buf.at[rows], hbm.at[rows], out_sem.at[a * n_piece + c])
            )
            outs[-1].start()

    @pl.when(has_down)
    def _():
        far_keep.wait_send()
        for a in range(3):
            for c in range(n_piece):
                far_copy(a, c).wait_send()

    @pl.when(is_odd | has_up)
    def _():
        near_keep.wait_send()
        for a in range(3):
            for c in range(n_piece):
                near_own(a, c).wait_send()

    for c in ag_copies:
        c.wait_send()
    for c in outs:
        c.wait()


def shards(params, gradients, moment_one, moment_two, keep_mask):
    features, rows_dev = params.shape
    blocks_dev = rows_dev // BLOCK
    sizes = tuple(lax.axis_size(a) for a in AXES)
    assert DROPS <= 2 * blocks_dev and sizes[2] % 2 == 0
    step = 16
    pieces = [(r, min(step, features - r)) for r in range(0, features, step)]
    full = jax.ShapeDtypeStruct((features, rows_dev), jnp.float32)
    plain = pltpu.VMEM((features, rows_dev), jnp.float32)
    window = [pltpu.VMEM((rows, 3 * rows_dev), jnp.float32) for _, rows in pieces]
    n_piece = len(pieces)
    n_ag = 2 * (sum(sizes) - 3)
    any_spec = pl.BlockSpec(memory_space=pl.ANY)
    p1, m1, v1, rms = pl.pallas_call(
        functools.partial(kernel, sizes, pieces),
        out_shape=(full, full, full, jax.ShapeDtypeStruct((1, 1), jnp.float32)),
        in_specs=[any_spec] * 5,
        out_specs=(any_spec, any_spec, any_spec, pl.BlockSpec(memory_space=pltpu.VMEM)),
        scratch_shapes=[
            [window, window, window], plain, plain, plain, plain, plain, plain,
            pltpu.VMEM((3, blocks_dev, BLOCK), jnp.int32),
            pltpu.VMEM((sizes[0], 8, BLOCK), jnp.float32),
            pltpu.VMEM((sizes[1], 8, BLOCK), jnp.float32),
            pltpu.VMEM((sizes[2], 8, BLOCK), jnp.float32),
            pltpu.VMEM((sizes[0], 8, BLOCK), jnp.int32),
            pltpu.VMEM((sizes[1], 8, BLOCK), jnp.int32),
            pltpu.VMEM((sizes[2], 8, BLOCK), jnp.int32),
            pltpu.VMEM((blocks_dev, BLOCK), jnp.int32),
            pltpu.SMEM((blocks_dev, BLOCK), jnp.int32),
            pltpu.SemaphoreType.DMA((4 + n_piece,)),
            pltpu.SemaphoreType.DMA((3 * n_piece,)),
            pltpu.SemaphoreType.DMA((3 * n_piece + 1,)),
            pltpu.SemaphoreType.DMA((3 * n_piece + 1,)),
            pltpu.SemaphoreType.DMA((3 * n_piece + 1,)),
            pltpu.SemaphoreType.DMA((3 * n_piece + 1,)),
            pltpu.SemaphoreType.DMA((n_ag,)),
            pltpu.SemaphoreType.DMA((n_ag,)),
            pltpu.SemaphoreType.DMA,
        ],
        compiler_params=pltpu.CompilerParams(
            collective_id=0, has_side_effects=True, vmem_limit_bytes=40 * 1024 * 1024
        ),
    )(params, gradients, moment_one, moment_two, keep_mask.reshape(blocks_dev, BLOCK))
    return p1, m1, v1, rms.reshape(())


def solution(mesh):
    spec = P(None, AXES)
    return jax.shard_map(
        shards, mesh=mesh, in_specs=(spec, spec, spec, spec, P(AXES)),
        out_specs=(spec, spec, spec, P()), check_vma=False,
    )
```

```python
import functools

import jax
import jax.numpy as jnp
from jax import lax
from jax.experimental import pallas as pl
from jax.experimental.pallas import tpu as pltpu
from jax.sharding import PartitionSpec as P

BLOCK = 128
ROWS = 8
DROPS = 32
STEP = 10
AXES = ("gx", "gy", "gz")
MESH = pl.DeviceIdType.MESH

beta_one = 0.9
beta_two = 0.999
learn_rate = 0.05
adam_eps = 1e-08
clip_rms = 1.0


def kernel(
    sizes, pieces, p_hbm, g_hbm, m_hbm, v_hbm, k_hbm, o_p, o_m, o_v, rms_ref,
    windows, tails, g_buf, m_buf, v_buf, p_rest, keep, ag_x, ag_y, ag_z, ct_x, ct_y, ct_z,
    where_v, where_s, load_sem, far_send, far_recv, near_send, near_recv,
    ag_send, ag_recv, where_sem,
):
    nx, ny, nz = sizes
    count = nx * ny * nz
    features, rows_dev = g_buf.shape
    blocks_dev = rows_dev // BLOCK
    n_piece = len(pieces)
    rest = p_rest.shape[0]
    top = features - rest
    ix, iy, iz = (lax.axis_index(a) for a in AXES)
    me = (ix * ny + iy) * nz + iz
    odd = lax.rem(me, 2)
    is_odd = odd == 1
    is_even = odd == 0
    has_up = me + 2 < count
    has_down = me >= 2

    def place(n):
        return (lax.div(n, ny * nz), lax.rem(lax.div(n, nz), ny), lax.rem(n, nz))

    partner = place(me + 1 - 2 * odd)
    below = place(lax.rem(me + count - 2, count))
    above = place(lax.rem(me + 2, count))
    own = pl.ds(0, rows_dev)

    def span(piece):
        return pl.ds(pieces[piece][0], pieces[piece][1])

    def load(i, src, dst):
        return pltpu.make_async_copy(src, dst, load_sem.at[i])

    loads = [
        load(0, g_hbm, g_buf),
        load(1, k_hbm, keep.at[0]),
        load(2, m_hbm, m_buf),
        load(3, v_hbm, v_buf),
    ] + [
        load(4 + c, p_hbm.at[span(c)], windows[0][c].at[:, own]) for c in range(len(pieces))
    ] + [load(4 + n_piece, p_hbm.at[pl.ds(top, rest)], p_rest)]
    for c in loads:
        c.start()

    barrier = pltpu.get_barrier_semaphore()

    def greet(device):
        pl.semaphore_signal(barrier, inc=1, device_id=device, device_id_type=MESH)

    groups = (
        (iz, nz, ag_z, ct_z, lambda i: (ix, iy, i)),
        (iy, ny, ag_y, ct_y, lambda i: (ix, i, iz)),
        (ix, nx, ag_x, ct_x, lambda i: (i, iy, iz)),
    )
    greet(partner)
    for mine, size, _, _, at in groups:
        for k in range(1, size):
            greet(at(lax.rem(mine + k, size)))
    pl.when(has_down)(lambda: greet(below))
    pl.when(has_up)(lambda: greet(above))

    loads[0].wait()
    loads[1].wait()
    g = g_buf[...]
    square = jnp.sum(g * g, axis=1, keepdims=True)
    square = jnp.sum(square, axis=0, keepdims=True)
    alive = (jnp.max(keep[0], axis=1, keepdims=True) > 0).astype(jnp.int32)
    payload = jnp.broadcast_to(square, (8, BLOCK))
    tally = jnp.broadcast_to(jnp.sum(alive, axis=0, keepdims=True), (8, BLOCK))

    pl.semaphore_wait(
        barrier,
        1 + (nx - 1) + (ny - 1) + (nz - 1) + has_up.astype(jnp.int32) + has_down.astype(jnp.int32),
    )

    def far(i, src, dst):
        return pltpu.make_async_remote_copy(
            src_ref=src, dst_ref=dst, send_sem=far_send.at[i], recv_sem=far_recv.at[i],
            device_id=below, device_id_type=MESH,
        )

    def near(i, src, dst):
        return pltpu.make_async_remote_copy(
            src_ref=src, dst_ref=dst, send_sem=near_send.at[i], recv_sem=near_recv.at[i],
            device_id=partner, device_id_type=MESH,
        )

    keep_id = 3 * n_piece + 3

    def place_of(a, c, slot):
        if c < n_piece:
            return windows[a][c].at[:, pl.ds(slot * rows_dev, rows_dev)]
        return tails[a].at[:, pl.ds(slot * blocks_dev, blocks_dev), :]

    def mine_of(a, c):
        return p_hbm.at[span(c)] if a == 0 and c < n_piece else place_of(a, c, 0)

    def far_copy(a, c):
        return far(a * (n_piece + 1) + c, mine_of(a, c), place_of(a, c, 2))

    def near_own(a, c):
        return near(a * (n_piece + 1) + c, mine_of(a, c), place_of(a, c, 1))

    def near_relay(a, c):
        return near(a * (n_piece + 1) + c, place_of(a, c, 2), place_of(a, c, 1))

    far_keep = far(keep_id, k_hbm, keep.at[2])
    near_keep = near(keep_id, k_hbm, keep.at[1])
    relay_keep = near(keep_id, keep.at[2], keep.at[1])

    def send(a, c):
        pl.when(has_down)(lambda: far_copy(a, c).start())
        pl.when(is_odd)(lambda: near_own(a, c).start())

    pl.when(has_down)(far_keep.start)
    pl.when(is_odd)(near_keep.start)

    def no_keep(i):
        keep[i] = jnp.zeros((blocks_dev, BLOCK), jnp.int32)

    pl.when(jnp.logical_not(has_up))(lambda: no_keep(2))
    pl.when(jnp.logical_not(has_up) & is_odd)(lambda: no_keep(1))

    before = jnp.zeros((8, BLOCK), jnp.int32)
    flow = list(range(n_piece))
    sem_at = 0
    ag_copies = []
    for phase, (mine, size, ag, ct, at) in enumerate(groups):
        ag[mine] = payload
        ct[mine] = tally
        copies = []
        for k in range(1, size):
            for buf in (ag, ct):
                copies.append(
                    pltpu.make_async_remote_copy(
                        src_ref=buf.at[mine], dst_ref=buf.at[mine],
                        send_sem=ag_send.at[sem_at], recv_sem=ag_recv.at[sem_at],
                        device_id=at(lax.rem(mine + k, size)), device_id_type=MESH,
                    )
                )
                copies[-1].start()
                sem_at += 1
        for _ in range(1 if phase < 2 else n_piece):
            if flow:
                send(0, flow.pop(0))
        for c in copies:
            c.wait_recv()
        ag_copies += copies
        payload, tally = ag[0], ct[0]
        for i in range(1, size):
            payload, tally = payload + ag[i], tally + ct[i]
        for i in range(size):
            before = before + jnp.where(i < mine, ct[i], 0)

    grad_rms = jnp.sqrt(payload[0:1, 0:1] / float(features * rows_dev * count))
    rms_ref[...] = grad_rms
    clip_factor = jnp.minimum(1.0, clip_rms / (grad_rms + 1e-06))

    loads[2].wait()
    loads[3].wait()
    kept = keep[0]
    kept = jnp.concatenate([kept[b : b + 1, :] for b in range(blocks_dev)], axis=1) > 0
    for c in range(n_piece):
        rows = span(c)
        clipped = clip_factor * g_buf[rows, :]
        first = beta_one * m_buf[rows, :] + (1.0 - beta_one) * clipped
        windows[1][c][:, own] = jnp.where(kept, first, 0.0)
        second = beta_two * v_buf[rows, :] + (1.0 - beta_two) * clipped * clipped
        windows[2][c][:, own] = jnp.where(kept, second, 0.0)
        send(1, c)
        send(2, c)
    loads[-1].wait()
    g_rest, m_rest, v_rest = (
        [x[top + r : top + r + 1, :] for r in range(rest)] for x in (g_buf, m_buf, v_buf)
    )

    def packed(row):
        return jnp.concatenate(
            [row[:, b * BLOCK : (b + 1) * BLOCK] for b in range(blocks_dev)], axis=0
        )

    for r in range(rest):
        kept = keep[0] > 0
        tails[0][r, 0:blocks_dev, :] = packed(p_rest[r : r + 1, :])
        clipped = clip_factor * packed(g_rest[r])
        first = beta_one * packed(m_rest[r]) + (1.0 - beta_one) * clipped
        tails[1][r, 0:blocks_dev, :] = jnp.where(kept, first, 0.0)
        second = beta_two * packed(v_rest[r]) + (1.0 - beta_two) * clipped * clipped
        tails[2][r, 0:blocks_dev, :] = jnp.where(kept, second, 0.0)
    for a in range(3):
        send(a, n_piece)

    @pl.when(has_up)
    def _():
        far_keep.wait_recv()

    @pl.when(is_even & has_up)
    def _():
        relay_keep.start()

    pl.when(is_even | has_up)(near_keep.wait_recv)
    total_blocks = 3 * blocks_dev
    flags = [(jnp.max(keep[i], axis=1, keepdims=True) > 0).astype(jnp.int32) for i in range(3)]
    flags = jnp.concatenate(flags, axis=0)
    up_to = lax.broadcasted_iota(jnp.int32, (total_blocks, BLOCK), 0) <= lax.broadcasted_iota(
        jnp.int32, (total_blocks, BLOCK), 1
    )
    reached = jnp.sum(
        jnp.where(up_to, jnp.broadcast_to(flags, (total_blocks, BLOCK)), 0), axis=0, keepdims=True
    )
    shift = me * blocks_dev - before[0:1, :]
    slot = lax.broadcasted_iota(jnp.int32, (blocks_dev, BLOCK), 0)
    lane = lax.broadcasted_iota(jnp.int32, (blocks_dev, BLOCK), 1)
    passed = (reached <= slot + shift) & (lane < total_blocks)
    index = jnp.sum(passed.astype(jnp.int32), axis=1, keepdims=True)
    where_v[...] = jnp.broadcast_to(index, (blocks_dev, BLOCK))
    to_scalar = pltpu.make_async_copy(where_v, where_s, where_sem)
    to_scalar.start()
    to_scalar.wait()
    for c in loads[4:-1]:
        c.wait()

    def relay(a, c):
        @pl.when(has_up)
        def _():
            far_copy(a, c).wait_recv()

        @pl.when(is_even & has_up)
        def _():
            near_relay(a, c).start()

    for c in range(n_piece):
        relay(0, c)

    correct_one = 1.0 - beta_one**STEP
    correct_two = 1.0 - beta_two**STEP
    def finish(j, valid, rows, old, first, second):
        dst = (rows, pl.ds(j * BLOCK, BLOCK))
        updated = old - learn_rate * (first / correct_one) / (
            jnp.sqrt(second / correct_two) + adam_eps
        )
        o_p[dst] = jnp.where(valid & (second > 0.0), updated, 0.0)
        o_m[dst] = jnp.where(valid, first, 0.0)
        o_v[dst] = jnp.where(valid, second, 0.0)

    for c in range(n_piece + 1):
        for a in range(3):
            if a > 0 or c == n_piece:
                relay(a, c)
        for a in range(3):
            pl.when(is_even | has_up)(near_own(a, c).wait_recv)
        for j in range(blocks_dev):
            block = where_s[j, 0]
            valid = block < total_blocks
            block = jnp.where(valid, block, 0)
            if c < n_piece:
                took = [windows[a][c][:, pl.ds(block * BLOCK, BLOCK)] for a in range(3)]
                finish(j, valid, span(c), *took)
            else:
                took = [
                    jnp.concatenate([tails[a][r, pl.ds(block, 1), :] for r in range(rest)], axis=0)
                    for a in range(3)
                ]
                finish(j, valid, pl.ds(top, rest), *took)

    @pl.when(has_down)
    def _():
        far_keep.wait_send()
        for a in range(3):
            for c in range(n_piece + 1):
                far_copy(a, c).wait_send()

    @pl.when(is_odd | has_up)
    def _():
        near_keep.wait_send()
        for a in range(3):
            for c in range(n_piece + 1):
                near_own(a, c).wait_send()

    for c in ag_copies:
        c.wait_send()


def put_kernel(a_in, b_in, c_in, a_out, b_out, c_out, sem):
    copies = [
        pltpu.make_async_copy(src, dst, sem.at[i])
        for i, (src, dst) in enumerate(((a_in, a_out), (b_in, b_out), (c_in, c_out)))
    ]
    for c in copies:
        c.start()
    for c in copies:
        c.wait()


def shards(params, gradients, moment_one, moment_two, keep_mask):
    features, rows_dev = params.shape
    blocks_dev = rows_dev // BLOCK
    sizes = tuple(lax.axis_size(a) for a in AXES)
    assert DROPS <= 2 * blocks_dev and sizes[2] % 2 == 0
    pieces = [(r, ROWS) for r in range(0, features - ROWS + 1, ROWS)]
    rest = features % ROWS
    assert rest and (rest * blocks_dev) % ROWS == 0
    full = jax.ShapeDtypeStruct((features, rows_dev), jnp.float32)
    plain = pltpu.VMEM((features, rows_dev), jnp.float32)
    window = [pltpu.VMEM((rows, 3 * rows_dev), jnp.float32) for _, rows in pieces]
    tail = pltpu.VMEM((rest, 3 * blocks_dev, BLOCK), jnp.float32)
    n_piece = len(pieces)
    n_ag = 2 * (sum(sizes) - 3)
    any_spec = pl.BlockSpec(memory_space=pl.ANY)
    p1, m1, v1, rms = pl.pallas_call(
        functools.partial(kernel, sizes, pieces),
        out_shape=(full, full, full, jax.ShapeDtypeStruct((1, 1), jnp.float32)),
        in_specs=[pl.BlockSpec(memory_space=pltpu.HBM)] * 5,
        out_specs=(pl.BlockSpec(memory_space=pltpu.VMEM),) * 4,
        scratch_shapes=[
            [window, window, window], [tail, tail, tail], plain, plain, plain, pltpu.VMEM((rest, rows_dev), jnp.float32),
            pltpu.VMEM((3, blocks_dev, BLOCK), jnp.int32),
            pltpu.VMEM((sizes[0], 8, BLOCK), jnp.float32),
            pltpu.VMEM((sizes[1], 8, BLOCK), jnp.float32),
            pltpu.VMEM((sizes[2], 8, BLOCK), jnp.float32),
            pltpu.VMEM((sizes[0], 8, BLOCK), jnp.int32),
            pltpu.VMEM((sizes[1], 8, BLOCK), jnp.int32),
            pltpu.VMEM((sizes[2], 8, BLOCK), jnp.int32),
            pltpu.VMEM((blocks_dev, BLOCK), jnp.int32),
            pltpu.SMEM((blocks_dev, BLOCK), jnp.int32),
            pltpu.SemaphoreType.DMA((5 + n_piece,)),
            pltpu.SemaphoreType.DMA((3 * n_piece + 4,)),
            pltpu.SemaphoreType.DMA((3 * n_piece + 4,)),
            pltpu.SemaphoreType.DMA((3 * n_piece + 4,)),
            pltpu.SemaphoreType.DMA((3 * n_piece + 4,)),
            pltpu.SemaphoreType.DMA((n_ag,)),
            pltpu.SemaphoreType.DMA((n_ag,)),
            pltpu.SemaphoreType.DMA,
        ],
        compiler_params=pltpu.CompilerParams(
            collective_id=0, has_side_effects=True, vmem_limit_bytes=40 * 1024 * 1024
        ),
    )(*(pltpu.with_memory_space_constraint(x, pltpu.HBM) for x in (params, gradients, moment_one, moment_two, keep_mask.reshape(blocks_dev, BLOCK))))
    p1, m1, v1 = pl.pallas_call(
        put_kernel,
        out_shape=(full, full, full),
        in_specs=[pl.BlockSpec(memory_space=pltpu.VMEM)] * 3,
        out_specs=(pl.BlockSpec(memory_space=pltpu.HBM),) * 3,
        scratch_shapes=[pltpu.SemaphoreType.DMA((3,))],
    )(*(pltpu.with_memory_space_constraint(x, pltpu.VMEM) for x in (p1, m1, v1)))
    return p1, m1, v1, rms.reshape(())


def solution(mesh):
    spec = P(None, AXES)
    return jax.shard_map(
        shards, mesh=mesh, in_specs=(spec, spec, spec, spec, P(AXES)),
        out_specs=(spec, spec, spec, P()), check_vma=False,
    )
```

```python
import functools

import jax
import jax.numpy as jnp
from jax import lax
from jax.experimental import pallas as pl
from jax.experimental.pallas import tpu as pltpu
from jax.sharding import PartitionSpec as P

BLOCK = 128
ROWS = 8
DROPS = 32
STEP = 10
AXES = ("gx", "gy", "gz")
MESH = pl.DeviceIdType.MESH

beta_one = 0.9
beta_two = 0.999
learn_rate = 0.05
adam_eps = 1e-08
clip_rms = 1.0


def kernel(
    sizes, pieces, p_hbm, g_hbm, m_hbm, v_hbm, k_hbm, o_p, o_m, o_v, rms_ref,
    windows, tails, g_buf, m_buf, v_buf, p_rest, keep, ag_x, ag_y, ct_x, ct_y,
    where_v, where_s, load_sem, far_send, far_recv, near_send, near_recv,
    ag_send, ag_recv, where_sem,
):
    nx, ny, nz = sizes
    count = nx * ny * nz
    features, rows_dev = g_buf.shape
    blocks_dev = rows_dev // BLOCK
    n_piece = len(pieces)
    rest = p_rest.shape[0]
    top = features - rest
    ix, iy, iz = (lax.axis_index(a) for a in AXES)
    me = (ix * ny + iy) * nz + iz
    odd = lax.rem(me, 2)
    is_odd = odd == 1
    is_even = odd == 0
    has_up = me + 2 < count
    has_down = me >= 2

    def place(n):
        return (lax.div(n, ny * nz), lax.rem(lax.div(n, nz), ny), lax.rem(n, nz))

    partner = place(me + 1 - 2 * odd)
    below = place(lax.rem(me + count - 2, count))
    above = place(lax.rem(me + 2, count))
    own = pl.ds(0, rows_dev)

    def span(piece):
        return pl.ds(pieces[piece][0], pieces[piece][1])

    def load(i, src, dst):
        return pltpu.make_async_copy(src, dst, load_sem.at[i])

    loads = [
        load(0, g_hbm, g_buf),
        load(1, k_hbm, keep.at[0]),
        load(2, m_hbm, m_buf),
        load(3, v_hbm, v_buf),
    ] + [
        load(4 + c, p_hbm.at[span(c)], windows[0][c].at[:, own]) for c in range(len(pieces))
    ] + [load(4 + n_piece, p_hbm.at[pl.ds(top, rest)], p_rest)]
    for c in loads:
        c.start()

    barrier = pltpu.get_barrier_semaphore()

    def greet(device):
        pl.semaphore_signal(barrier, inc=1, device_id=device, device_id_type=MESH)

    groups = (
        (iy * nz + iz, ny * nz, ag_y, ct_y, lambda i: (ix, lax.div(i, nz), lax.rem(i, nz))),
        (ix, nx, ag_x, ct_x, lambda i: (i, iy, iz)),
    )
    greet(partner)
    for mine, size, _, _, at in groups:
        for k in range(1, size):
            greet(at(lax.rem(mine + k, size)))
    pl.when(has_down)(lambda: greet(below))
    pl.when(has_up)(lambda: greet(above))

    loads[0].wait()
    loads[1].wait()
    g = g_buf[...]
    square = jnp.sum(g * g, axis=1, keepdims=True)
    square = jnp.sum(square, axis=0, keepdims=True)
    alive = (jnp.max(keep[0], axis=1, keepdims=True) > 0).astype(jnp.int32)
    payload = jnp.broadcast_to(square, (8, BLOCK))
    tally = jnp.broadcast_to(jnp.sum(alive, axis=0, keepdims=True), (8, BLOCK))

    pl.semaphore_wait(
        barrier,
        1 + (nx - 1) + (ny * nz - 1) + has_up.astype(jnp.int32) + has_down.astype(jnp.int32),
    )

    def far(i, src, dst):
        return pltpu.make_async_remote_copy(
            src_ref=src, dst_ref=dst, send_sem=far_send.at[i], recv_sem=far_recv.at[i],
            device_id=below, device_id_type=MESH,
        )

    def near(i, src, dst):
        return pltpu.make_async_remote_copy(
            src_ref=src, dst_ref=dst, send_sem=near_send.at[i], recv_sem=near_recv.at[i],
            device_id=partner, device_id_type=MESH,
        )

    keep_id = 3 * n_piece + 3

    def place_of(a, c, slot):
        if c < n_piece:
            return windows[a][c].at[:, pl.ds(slot * rows_dev, rows_dev)]
        return tails[a].at[:, pl.ds(slot * blocks_dev, blocks_dev), :]

    def mine_of(a, c):
        return p_hbm.at[span(c)] if a == 0 and c < n_piece else place_of(a, c, 0)

    def far_copy(a, c):
        return far(a * (n_piece + 1) + c, mine_of(a, c), place_of(a, c, 2))

    def near_own(a, c):
        return near(a * (n_piece + 1) + c, mine_of(a, c), place_of(a, c, 1))

    def near_relay(a, c):
        return near(a * (n_piece + 1) + c, place_of(a, c, 2), place_of(a, c, 1))

    far_keep = far(keep_id, k_hbm, keep.at[2])
    near_keep = near(keep_id, k_hbm, keep.at[1])
    relay_keep = near(keep_id, keep.at[2], keep.at[1])

    def send(a, c):
        pl.when(has_down)(lambda: far_copy(a, c).start())
        pl.when(is_odd)(lambda: near_own(a, c).start())

    pl.when(has_down)(far_keep.start)
    pl.when(is_odd)(near_keep.start)

    def no_keep(i):
        keep[i] = jnp.zeros((blocks_dev, BLOCK), jnp.int32)

    pl.when(jnp.logical_not(has_up))(lambda: no_keep(2))
    pl.when(jnp.logical_not(has_up) & is_odd)(lambda: no_keep(1))

    before = jnp.zeros((8, BLOCK), jnp.int32)
    flow = list(range(n_piece))
    sem_at = 0
    ag_copies = []
    for phase, (mine, size, ag, ct, at) in enumerate(groups):
        ag[mine] = payload
        ct[mine] = tally
        copies = []
        for k in range(1, size):
            for buf in (ag, ct):
                copies.append(
                    pltpu.make_async_remote_copy(
                        src_ref=buf.at[mine], dst_ref=buf.at[mine],
                        send_sem=ag_send.at[sem_at], recv_sem=ag_recv.at[sem_at],
                        device_id=at(lax.rem(mine + k, size)), device_id_type=MESH,
                    )
                )
                copies[-1].start()
                sem_at += 1
        for _ in range((2, n_piece)[phase]):
            if flow:
                send(0, flow.pop(0))
        for c in copies:
            c.wait_recv()
        ag_copies += copies
        payload, tally = ag[0], ct[0]
        for i in range(1, size):
            payload, tally = payload + ag[i], tally + ct[i]
        for i in range(size):
            before = before + jnp.where(i < mine, ct[i], 0)

    grad_rms = jnp.sqrt(payload[0:1, 0:1] / float(features * rows_dev * count))
    rms_ref[...] = grad_rms
    clip_factor = jnp.minimum(1.0, clip_rms / (grad_rms + 1e-06))

    loads[2].wait()
    loads[3].wait()
    kept = keep[0]
    kept = jnp.concatenate([kept[b : b + 1, :] for b in range(blocks_dev)], axis=1) > 0
    for c in range(n_piece):
        rows = span(c)
        clipped = clip_factor * g_buf[rows, :]
        first = beta_one * m_buf[rows, :] + (1.0 - beta_one) * clipped
        windows[1][c][:, own] = jnp.where(kept, first, 0.0)
        second = beta_two * v_buf[rows, :] + (1.0 - beta_two) * clipped * clipped
        windows[2][c][:, own] = jnp.where(kept, second, 0.0)
        send(1, c)
        send(2, c)
    loads[-1].wait()
    g_rest, m_rest, v_rest = (
        [x[top + r : top + r + 1, :] for r in range(rest)] for x in (g_buf, m_buf, v_buf)
    )

    def packed(row):
        return jnp.concatenate(
            [row[:, b * BLOCK : (b + 1) * BLOCK] for b in range(blocks_dev)], axis=0
        )

    for r in range(rest):
        kept = keep[0] > 0
        tails[0][r, 0:blocks_dev, :] = packed(p_rest[r : r + 1, :])
        clipped = clip_factor * packed(g_rest[r])
        first = beta_one * packed(m_rest[r]) + (1.0 - beta_one) * clipped
        tails[1][r, 0:blocks_dev, :] = jnp.where(kept, first, 0.0)
        second = beta_two * packed(v_rest[r]) + (1.0 - beta_two) * clipped * clipped
        tails[2][r, 0:blocks_dev, :] = jnp.where(kept, second, 0.0)
    for a in range(3):
        send(a, n_piece)

    @pl.when(has_up)
    def _():
        far_keep.wait_recv()

    @pl.when(is_even & has_up)
    def _():
        relay_keep.start()

    pl.when(is_even | has_up)(near_keep.wait_recv)
    total_blocks = 3 * blocks_dev
    flags = [(jnp.max(keep[i], axis=1, keepdims=True) > 0).astype(jnp.int32) for i in range(3)]
    flags = jnp.concatenate(flags, axis=0)
    up_to = lax.broadcasted_iota(jnp.int32, (total_blocks, BLOCK), 0) <= lax.broadcasted_iota(
        jnp.int32, (total_blocks, BLOCK), 1
    )
    reached = jnp.sum(
        jnp.where(up_to, jnp.broadcast_to(flags, (total_blocks, BLOCK)), 0), axis=0, keepdims=True
    )
    shift = me * blocks_dev - before[0:1, :]
    slot = lax.broadcasted_iota(jnp.int32, (blocks_dev, BLOCK), 0)
    lane = lax.broadcasted_iota(jnp.int32, (blocks_dev, BLOCK), 1)
    passed = (reached <= slot + shift) & (lane < total_blocks)
    index = jnp.sum(passed.astype(jnp.int32), axis=1, keepdims=True)
    where_v[...] = jnp.broadcast_to(index, (blocks_dev, BLOCK))
    to_scalar = pltpu.make_async_copy(where_v, where_s, where_sem)
    to_scalar.start()
    to_scalar.wait()
    for c in loads[4:-1]:
        c.wait()

    def relay(a, c):
        @pl.when(has_up)
        def _():
            far_copy(a, c).wait_recv()

        @pl.when(is_even & has_up)
        def _():
            near_relay(a, c).start()

    for c in range(n_piece):
        relay(0, c)

    correct_one = 1.0 - beta_one**STEP
    correct_two = 1.0 - beta_two**STEP
    def finish(j, valid, rows, old, first, second):
        dst = (rows, pl.ds(j * BLOCK, BLOCK))
        updated = old - learn_rate * (first / correct_one) / (
            jnp.sqrt(second / correct_two) + adam_eps
        )
        o_p[dst] = jnp.where(valid & (second > 0.0), updated, 0.0)
        o_m[dst] = jnp.where(valid, first, 0.0)
        o_v[dst] = jnp.where(valid, second, 0.0)

    for c in range(n_piece + 1):
        for a in range(3):
            if a > 0 or c == n_piece:
                relay(a, c)
        for a in range(3):
            pl.when(is_even | has_up)(near_own(a, c).wait_recv)
        for j in range(blocks_dev):
            block = where_s[j, 0]
            valid = block < total_blocks
            block = jnp.where(valid, block, 0)
            if c < n_piece:
                took = [windows[a][c][:, pl.ds(block * BLOCK, BLOCK)] for a in range(3)]
                finish(j, valid, span(c), *took)
            else:
                took = [
                    jnp.concatenate([tails[a][r, pl.ds(block, 1), :] for r in range(rest)], axis=0)
                    for a in range(3)
                ]
                finish(j, valid, pl.ds(top, rest), *took)

    @pl.when(has_down)
    def _():
        far_keep.wait_send()
        for a in range(3):
            for c in range(n_piece + 1):
                far_copy(a, c).wait_send()

    @pl.when(is_odd | has_up)
    def _():
        near_keep.wait_send()
        for a in range(3):
            for c in range(n_piece + 1):
                near_own(a, c).wait_send()

    for c in ag_copies:
        c.wait_send()


def put_kernel(a_in, b_in, c_in, a_out, b_out, c_out, sem):
    copies = [
        pltpu.make_async_copy(src, dst, sem.at[i])
        for i, (src, dst) in enumerate(((a_in, a_out), (b_in, b_out), (c_in, c_out)))
    ]
    for c in copies:
        c.start()
    for c in copies:
        c.wait()


def shards(params, gradients, moment_one, moment_two, keep_mask):
    features, rows_dev = params.shape
    blocks_dev = rows_dev // BLOCK
    sizes = tuple(lax.axis_size(a) for a in AXES)
    assert DROPS <= 2 * blocks_dev and sizes[2] % 2 == 0
    whole = features // ROWS
    widths = [1] * whole if whole < 4 else [2] + [1] * (whole - 4) + [2]
    pieces = [(sum(widths[:i]) * ROWS, w * ROWS) for i, w in enumerate(widths)]
    rest = features % ROWS
    assert rest and (rest * blocks_dev) % ROWS == 0
    full = jax.ShapeDtypeStruct((features, rows_dev), jnp.float32)
    plain = pltpu.VMEM((features, rows_dev), jnp.float32)
    window = [pltpu.VMEM((rows, 3 * rows_dev), jnp.float32) for _, rows in pieces]
    tail = pltpu.VMEM((rest, 3 * blocks_dev, BLOCK), jnp.float32)
    n_piece = len(pieces)
    n_ag = 2 * (sizes[0] - 1 + sizes[1] * sizes[2] - 1)
    any_spec = pl.BlockSpec(memory_space=pl.ANY)
    p1, m1, v1, rms = pl.pallas_call(
        functools.partial(kernel, sizes, pieces),
        out_shape=(full, full, full, jax.ShapeDtypeStruct((1, 1), jnp.float32)),
        in_specs=[pl.BlockSpec(memory_space=pltpu.HBM)] * 5,
        out_specs=(pl.BlockSpec(memory_space=pltpu.VMEM),) * 4,
        scratch_shapes=[
            [window, window, window], [tail, tail, tail], plain, plain, plain, pltpu.VMEM((rest, rows_dev), jnp.float32),
            pltpu.VMEM((3, blocks_dev, BLOCK), jnp.int32),
            pltpu.VMEM((sizes[0], 8, BLOCK), jnp.float32),
            pltpu.VMEM((sizes[1] * sizes[2], 8, BLOCK), jnp.float32),
            pltpu.VMEM((sizes[0], 8, BLOCK), jnp.int32),
            pltpu.VMEM((sizes[1] * sizes[2], 8, BLOCK), jnp.int32),
            pltpu.VMEM((blocks_dev, BLOCK), jnp.int32),
            pltpu.SMEM((blocks_dev, BLOCK), jnp.int32),
            pltpu.SemaphoreType.DMA((5 + n_piece,)),
            pltpu.SemaphoreType.DMA((3 * n_piece + 4,)),
            pltpu.SemaphoreType.DMA((3 * n_piece + 4,)),
            pltpu.SemaphoreType.DMA((3 * n_piece + 4,)),
            pltpu.SemaphoreType.DMA((3 * n_piece + 4,)),
            pltpu.SemaphoreType.DMA((n_ag,)),
            pltpu.SemaphoreType.DMA((n_ag,)),
            pltpu.SemaphoreType.DMA,
        ],
        compiler_params=pltpu.CompilerParams(
            collective_id=0, has_side_effects=True, vmem_limit_bytes=40 * 1024 * 1024
        ),
    )(*(pltpu.with_memory_space_constraint(x, pltpu.HBM) for x in (params, gradients, moment_one, moment_two, keep_mask.reshape(blocks_dev, BLOCK))))
    p1, m1, v1 = pl.pallas_call(
        put_kernel,
        out_shape=(full, full, full),
        in_specs=[pl.BlockSpec(memory_space=pltpu.VMEM)] * 3,
        out_specs=(pl.BlockSpec(memory_space=pltpu.HBM),) * 3,
        scratch_shapes=[pltpu.SemaphoreType.DMA((3,))],
    )(*(pltpu.with_memory_space_constraint(x, pltpu.VMEM) for x in (p1, m1, v1)))
    return p1, m1, v1, rms.reshape(())


def solution(mesh):
    spec = P(None, AXES)
    return jax.shard_map(
        shards, mesh=mesh, in_specs=(spec, spec, spec, spec, P(AXES)),
        out_specs=(spec, spec, spec, P()), check_vma=False,
    )
```
